32 devices in a mesh: tm: 16 (over z, y, x), space: 2 (over core).
Axes of the slice: x: 2, y: 2, z: 4, core: 2. Of those that a mesh axis runs over, the one named last changes fastest.
Arguments:
- snapshots: bfloat16 [8192, 16384], P('tm', 'space'), may hold values from -40 to 40
- exponents: float32 [2, 32], replicated, may hold values from -150 to 150, as said below
Outputs:
- new_exponents: float32 [2, 32], replicated
- amplitudes: float32 [2, 32, 16384], P(None, None, 'space')
- residual: bfloat16 [8192, 16384], P('tm', 'space')
The draws below stay inside these ranges and needn't reach their ends.
Inputs may be any that keep to these rules, and one draw needn't show every extreme that they name: `exponents`: row 0 lies in -2.3 to 0.8, row 1 in -150 to 150.
All inputs are finite; a program needn't handle non-finite values.
Results may differ from the reference program's by a relative error of at most 0.0012.
The reference program's roundings to bfloat16 on the way count: a program that leaves them out, or rounds other values in their place, can miss the bound.
Values sent between devices are 32-bit elements; how exact they have to be, the bound alone decides.
A program may use at most 64 MiB of HBM per device.

```python
import math
import jax
import jax.numpy as jnp
from jax import lax

MODES = 32
TIMES = 8192
SPACE = 16384


def true_modes(key):
    base = jax.random.fold_in(key, 7)
    first_key, second_key = jax.random.split(base)
    decay_rates = jax.random.uniform(first_key, (MODES,), jnp.float32, -2.0, 0.5)
    spacing = 2.0 * math.pi * 1.5
    frequencies = spacing * (jnp.arange(MODES, dtype=jnp.float32) - (MODES - 1) / 2.0)
    frequencies = frequencies + jax.random.uniform(second_key, (MODES,), jnp.float32, -2.0, 2.0)
    return (decay_rates, frequencies)


def draw_exponents(key, part):
    decay_rates, frequencies = true_modes(key)
    first_key, second_key = jax.random.split(jax.random.fold_in(key, 19))
    shifted_rates = decay_rates + jax.random.uniform(first_key, (MODES,), jnp.float32, -0.3, 0.3)
    shifted_freqs = frequencies + jax.random.uniform(second_key, (MODES,), jnp.float32, -0.5, 0.5)
    return jnp.stack([shifted_rates, shifted_freqs]).astype(jnp.float32)


def draw_snapshots(key, part):
    decay_rates, frequencies = true_modes(key)
    time_grid = jnp.arange(TIMES, dtype=jnp.int32).astype(jnp.float32) / TIMES
    first_key, second_key = jax.random.split(jax.random.fold_in(key, 23))
    column_pos = jnp.arange(SPACE, dtype=jnp.int32).astype(jnp.float32) / SPACE
    column_scale = 0.15 * (1.0 + 2.0 * column_pos)
    amp_real = jax.random.normal(first_key, (MODES, SPACE), jnp.float32) * column_scale[None, :]
    amp_imag = jax.random.normal(second_key, (MODES, SPACE), jnp.float32) * column_scale[None, :]
    region = jnp.arange(SPACE, dtype=jnp.int32) * 4 // SPACE
    model_part = jnp.zeros((TIMES, SPACE), jnp.float32)
    for quarter in range(4):
        offset = quarter - 1.5
        magnitude = jnp.exp(time_grid[:, None] * (decay_rates + 0.2 * offset)[None, :])
        phase_angle = time_grid[:, None] * (frequencies + 0.8 * offset)[None, :]
        inside = (region == quarter).astype(jnp.float32)[None, :]
        model_part = model_part + jnp.dot(magnitude * jnp.cos(phase_angle), amp_real * inside, precision=lax.Precision.HIGHEST)
        model_part = model_part - jnp.dot(magnitude * jnp.sin(phase_angle), amp_imag * inside, precision=lax.Precision.HIGHEST)
    noise_field = 0.5 * jax.random.normal(jax.random.fold_in(key, 29), (TIMES, SPACE), jnp.float32)
    return jnp.clip(model_part + noise_field, -40.0, 40.0).astype(jnp.bfloat16)


def setup_inputs(seed: int = 0) -> dict:
    key_of = jax.random.split(jax.random.key(seed), 3)
    return {
        "snapshots": draw_snapshots(jax.random.fold_in(key_of[2], 71), 0),
        "exponents": draw_exponents(jax.random.fold_in(key_of[2], 71), 0),
    }


damping = 0.01

def factor_solve(factor, right):
    lower_part = lax.linalg.triangular_solve(factor, right, left_side=True, lower=True)
    return lax.linalg.triangular_solve(factor, lower_part, left_side=True, lower=True, transpose_a=True)

def make_basis(exponents, time_grid):
    magnitude = jnp.exp(time_grid[:, None] * exponents[0][None, :])
    phase_angle = time_grid[:, None] * exponents[1][None, :]
    plain = jnp.concatenate([magnitude * jnp.cos(phase_angle), magnitude * jnp.sin(phase_angle)], 1)
    return jnp.concatenate([plain, time_grid[:, None] * plain], 1)

def inner_product(left, right):
    return lax.dot_general(left.astype(jnp.float32), right.astype(jnp.float32), (((0,), (0,)), ((), ())), precision=lax.Precision.HIGHEST, preferred_element_type=jnp.float32)

def hermitian(blocks, modes):
    return (blocks[:modes, :modes] + blocks[modes:, modes:], blocks[:modes, modes:] - blocks[modes:, :modes])

def embedded(real_part, imag_part):
    return jnp.concatenate([jnp.concatenate([real_part, -imag_part], 1), jnp.concatenate([imag_part, real_part], 1)], 0)

def sign_flip(modes):
    return jnp.concatenate([jnp.ones((modes,), jnp.float32), -jnp.ones((modes,), jnp.float32)])

def basis_solve(gram_matrix, modes):
    double = 2 * modes
    g_real, g_imag = hermitian(gram_matrix[:double, :double], modes)
    factor = jnp.linalg.cholesky(embedded(g_real, g_imag))
    return factor_solve(factor, jnp.eye(double, dtype=jnp.float32))

def amplitude_rows(inverse_g, projections, modes):
    left_solve = inverse_g * sign_flip(modes)[None, :]
    return lax.dot_general(left_solve.astype(jnp.float32), projections[:, :2 * modes].astype(jnp.float32), (((1,), (1,)), ((), ())), precision=lax.Precision.HIGHEST, preferred_element_type=jnp.float32)

def fit_terms(amp_rows, projections, modes):
    double = 2 * modes
    self_terms = lax.dot_general(amp_rows.astype(jnp.float32), amp_rows.astype(jnp.float32), (((1,), (1,)), ((), ())), precision=lax.Precision.HIGHEST, preferred_element_type=jnp.float32)
    cross = jnp.dot(amp_rows.astype(jnp.float32), projections[:, double:].astype(jnp.float32), precision=lax.Precision.HIGHEST, preferred_element_type=jnp.float32) * sign_flip(modes)[None, :]
    v_real = jnp.diagonal(cross[:modes, :modes]) + jnp.diagonal(cross[modes:, modes:])
    v_imag = jnp.diagonal(cross[:modes, modes:]) - jnp.diagonal(cross[modes:, :modes])
    return (self_terms, jnp.stack([v_real, v_imag]))

def lm_update(exponents, gram_matrix, inverse_g, self_terms, cross_sums, modes):
    double = 2 * modes
    c_real, c_imag = hermitian(gram_matrix[:double, double:], modes)
    e_real, e_imag = hermitian(gram_matrix[double:, double:], modes)
    coupling = embedded(c_real, c_imag)
    through = jnp.dot(coupling.T, inverse_g, precision=lax.Precision.HIGHEST)
    reduced = embedded(e_real, e_imag) - jnp.dot(through, coupling, precision=lax.Precision.HIGHEST)
    m_real = reduced[:modes, :modes]
    m_imag = reduced[modes:, :modes]
    s_real, s_imag = hermitian(self_terms, modes)
    w_real = jnp.sum(c_real.T * s_real + c_imag.T * s_imag, 1)
    w_imag = jnp.sum(c_real.T * s_imag - c_imag.T * s_real, 1)
    grad_real = w_real - cross_sums[0]
    grad_imag = w_imag - cross_sums[1]
    h_real = s_real * m_real - s_imag * m_imag + damping * jnp.eye(modes, dtype=jnp.float32)
    h_imag = s_real * m_imag + s_imag * m_real
    factor = jnp.linalg.cholesky(embedded(h_real, h_imag))
    step_vector = factor_solve(factor, jnp.concatenate([grad_real, grad_imag])[:, None])[:, 0]
    return exponents - jnp.stack([step_vector[:modes], step_vector[modes:]])

def reference(snapshots, exponents):
    modes = MODES
    time_grid = jnp.arange(TIMES, dtype=jnp.int32).astype(jnp.float32) / TIMES
    basis = make_basis(exponents, time_grid)
    gram_matrix = inner_product(basis, basis)
    basis_b = basis.astype(jnp.bfloat16)
    projections = lax.dot_general(snapshots.astype(jnp.float32), basis_b.astype(jnp.float32), (((0,), (0,)), ((), ())), preferred_element_type=jnp.float32)
    inverse_g = basis_solve(gram_matrix, modes)
    amp_rows = amplitude_rows(inverse_g, projections, modes)
    self_terms, cross_sums = fit_terms(amp_rows, projections, modes)
    new_exponents = lm_update(exponents, gram_matrix, inverse_g, self_terms, cross_sums, modes)
    signed = (amp_rows * sign_flip(modes)[:, None]).astype(jnp.bfloat16)
    fitted = jnp.dot(basis_b[:, :2 * modes].astype(jnp.float32), signed.astype(jnp.float32), preferred_element_type=jnp.float32)
    residual = (snapshots.astype(jnp.float32) - fitted).astype(jnp.bfloat16)
    return (new_exponents, amp_rows.reshape(2, modes, SPACE), residual)
```

```python
import functools

import jax
import jax.numpy as jnp
from jax import lax
from jax.experimental import pallas as pl
from jax.experimental.pallas import tpu as pltpu
from jax.sharding import PartitionSpec as P

damping = 0.01
MESH = pl.DeviceIdType.MESH
LANES = 128
ORDERS = ((0, 1, 2), (1, 0, 2), (2, 0, 1), (1, 2, 0))


def exact_dot(left, right, dims=((1,), (0,))):
    return lax.dot_general(
        left,
        right,
        (dims, ((), ())),
        precision=lax.Precision.HIGHEST,
        preferred_element_type=jnp.float32,
    )


def complex_inverse(real, imag):
    modes = real.shape[0]
    rows = lax.broadcasted_iota(jnp.int32, real.shape, 0)
    cols = lax.broadcasted_iota(jnp.int32, real.shape, 1)
    for k in range(modes):
        on_row, on_col = rows == k, cols == k
        scale = 1.0 / real[k : k + 1, k : k + 1]
        row_r = jnp.where(on_col[:1], 1.0, real[k : k + 1, :]) * scale
        row_i = jnp.where(on_col[:1], 0.0, imag[k : k + 1, :]) * scale
        col_r, col_i = real[:, k : k + 1], imag[:, k : k + 1]
        real = jnp.where(
            on_row, row_r, jnp.where(on_col, 0.0, real) - (col_r * row_r - col_i * row_i)
        )
        imag = jnp.where(
            on_row, row_i, jnp.where(on_col, 0.0, imag) - (col_r * row_i + col_i * row_r)
        )
    return real, imag


def complex_dot(ar, ai, br, bi):
    return exact_dot(ar, br) - exact_dot(ai, bi), exact_dot(ar, bi) + exact_dot(ai, br)


def exchange_kernel(
    modes, tm_bits, sp_bits, parts,
    yz_ref, gram_ref, exps_ref,
    amp_ref, new_ref,
    full, halves, gsum, grecv, ssum, srecv, vsum, vrecv,
    rs_send, rs_recv, ag_send, ag_recv,
    g_send, g_recv, s_send, s_recv, v_send, v_recv, out_sem,
):
    double = 2 * modes
    columns = full.shape[1]
    width = columns // parts
    me, sp = lax.axis_index("tm"), lax.axis_index("space")
    swap = sp % 2

    def stride_of(bit):
        if tm_bits >= 2 and bit == 0:
            return 1 + swap
        if tm_bits >= 2 and bit == 1:
            return 2 - swap
        return 2**bit

    def flip(index, stride):
        side = (index // stride) % 2
        return side, index + (1 - 2 * side) * stride

    friends = [(flip(me, 2**b)[1], sp) for b in range(tm_bits)]
    friends += [(me, flip(sp, 2**b)[1]) for b in range(sp_bits)]

    barrier = pltpu.get_barrier_semaphore()
    for friend in friends:
        pl.semaphore_signal(barrier, inc=1, device_id=friend, device_id_type=MESH)
    pl.semaphore_wait(barrier, len(friends))

    def remote(src, dst, send, recv, friend):
        copy = pltpu.make_async_remote_copy(
            src_ref=src, dst_ref=dst, send_sem=send, recv_sem=recv,
            device_id=friend, device_id_type=MESH,
        )
        copy.start()
        return copy

    sends = []

    def sum_start(stage, total, landed, send, recv):
        copy = remote(
            total.at[stage], landed.at[stage], send.at[stage], recv.at[stage], friends[stage]
        )
        sends.append(copy)
        return copy

    def sum_end(stage, copy, total, landed):
        copy.wait_recv()
        total[stage + 1] = total[stage] + landed[stage]

    plan = []
    for p in range(parts):
        first = [b for b in ORDERS[p % len(ORDERS)] if b < tm_bits]
        order = first + [b for b in range(tm_bits) if b not in first]
        plan.append([flip(me, stride_of(b)) for b in order])

    def lanes(start, size):
        return pl.ds(pl.multiple_of(start, LANES), size)

    def scatter_start(p, s):
        side, partner = plan[p][s]
        size = width >> (s + 1)
        away = (1 - side) * size
        if s == 0:
            src = yz_ref.at[pl.ds(0, double), lanes(p * width + away, size)]
        else:
            src = halves[s - 1].at[p, :, lanes(away, size)]
        copy = remote(src, halves[s].at[p], rs_send.at[p, s], rs_recv.at[p, s], (partner, sp))
        sends.append(copy)
        return copy

    def scatter_add(p, s):
        side, _ = plan[p][s]
        size = width >> (s + 1)
        keep = side * size
        if s == 0:
            mine = yz_ref[pl.ds(0, double), lanes(p * width + keep, size)]
        else:
            mine = halves[s - 1][p, :, lanes(keep, size)]
        halves[s][p] = halves[s][p] + mine

    gsum[0] = gram_ref[...]
    flying = [scatter_start(p, 0) for p in range(parts)]
    g_copy = sum_start(0, gsum, grecv, g_send, g_recv)
    for s in range(tm_bits):
        sum_end(s, g_copy, gsum, grecv)
        if s + 1 < tm_bits:
            g_copy = sum_start(s + 1, gsum, grecv, g_send, g_recv)
            for p in range(parts):
                flying[p].wait_recv()
                scatter_add(p, s)
                flying[p] = scatter_start(p, s + 1)

    blocks = gsum[tm_bits]

    def block(index):
        moved = blocks if index == 0 else pltpu.roll(blocks, LANES - index * modes, 1)
        return moved[:modes, :modes], moved[modes:, :modes]

    g_r, g_i = block(0)
    c_r, c_i = block(1)
    e_r, e_i = block(2)
    inv_r, inv_i = complex_inverse(g_r, g_i)
    t_r, t_i = complex_dot(inv_r, inv_i, c_r, c_i)
    u_r, u_i = complex_dot(c_r, c_i, t_r, t_i)
    m_r, m_i = e_r - u_r, e_i - u_i

    offsets = []
    self_r = jnp.zeros((modes, modes), jnp.float32)
    self_i = jnp.zeros((modes, modes), jnp.float32)
    last = tm_bits - 1

    def gather_start(p, s):
        size = width >> (s + 1)
        where = full.at[:, lanes(offsets[p], size)]
        _, partner = plan[p][s]
        copy = remote(where, where, ag_send.at[p, s], ag_recv.at[p, s], (partner, sp))
        sends.append(copy)
        return copy

    for p in range(parts):
        flying[p].wait_recv()
        scatter_add(p, last)
        own = halves[last][p]
        a_r, a_i = complex_dot(inv_r, inv_i, own[:modes], own[modes:])
        start = p * width
        for s in range(tm_bits):
            start = start + plan[p][s][0] * (width >> (s + 1))
        offsets.append(start)
        size = width >> tm_bits
        full[pl.ds(0, modes), lanes(start, size)] = a_r
        full[pl.ds(modes, modes), lanes(start, size)] = a_i
        flying[p] = gather_start(p, last)
        over = ((1,), (1,))
        self_r += exact_dot(a_r, a_r, over) + exact_dot(a_i, a_i, over)
        self_i += exact_dot(a_r, a_i, over) - exact_dot(a_i, a_r, over)

    ssum[0] = jnp.zeros(ssum.shape[1:], jnp.float32)
    ssum[0, pl.ds(0, modes), pl.ds(0, modes)] = self_r
    ssum[0, pl.ds(modes, modes), pl.ds(0, modes)] = self_i
    s_copy = sum_start(0, ssum, srecv, s_send, s_recv)
    s_stage = 0
    steps = len(friends)
    for s in range(last, 0, -1):
        sum_end(s_stage, s_copy, ssum, srecv)
        s_stage += 1
        s_copy = sum_start(s_stage, ssum, srecv, s_send, s_recv)
        for p in range(parts):
            flying[p].wait_recv()
            offsets[p] = offsets[p] - plan[p][s][0] * (width >> (s + 1))
            flying[p] = gather_start(p, s - 1)
    while s_stage < steps:
        sum_end(s_stage, s_copy, ssum, srecv)
        s_stage += 1
        if s_stage < steps:
            s_copy = sum_start(s_stage, ssum, srecv, s_send, s_recv)

    s_r = ssum[steps, pl.ds(0, modes), pl.ds(0, modes)]
    s_i = ssum[steps, pl.ds(modes, modes), pl.ds(0, modes)]
    square = (modes, modes)
    diagonal = lax.broadcasted_iota(jnp.int32, square, 0) == lax.broadcasted_iota(
        jnp.int32, square, 1
    )
    h_r = s_r * m_r - s_i * m_i + jnp.where(diagonal, damping, 0.0)
    h_i = s_r * m_i + s_i * m_r
    hinv_r, hinv_i = complex_inverse(h_r, h_i)
    w_r = jnp.sum(c_r * s_r - c_i * s_i, 1, keepdims=True)
    w_i = jnp.sum(c_r * s_i + c_i * s_r, 1, keepdims=True)

    v_r = jnp.zeros((modes, LANES), jnp.float32)
    v_i = jnp.zeros((modes, LANES), jnp.float32)
    outs = []
    for p in range(parts):
        flying[p].wait_recv()
        part = pl.ds(p * width, width)
        out = pltpu.make_async_copy(full.at[:, part], amp_ref.at[:, part], out_sem.at[p])
        out.start()
        outs.append(out)
        run = 4

        def step(i, carry, p=p):
            v_r, v_i = carry
            for j in range(run):
                at = lanes(p * width + (i * run + j) * LANES, LANES)
                a_r, a_i = full[pl.ds(0, modes), at], full[pl.ds(modes, modes), at]
                z_r = yz_ref[pl.ds(double, modes), at]
                z_i = yz_ref[pl.ds(double + modes, modes), at]
                v_r = v_r + (a_r * z_r + a_i * z_i)
                v_i = v_i + (a_r * z_i - a_i * z_r)
            return v_r, v_i

        v_r, v_i = lax.fori_loop(0, width // (run * LANES), step, (v_r, v_i))

    ones = jnp.ones((8, LANES), jnp.float32)
    vsum[0] = jnp.zeros(vsum.shape[1:], jnp.float32)
    vsum[0, pl.ds(0, 8), pl.ds(0, modes)] = exact_dot(ones, v_r, ((1,), (1,)))
    vsum[0, pl.ds(8, 8), pl.ds(0, modes)] = exact_dot(ones, v_i, ((1,), (1,)))
    for stage in range(steps):
        v_copy = sum_start(stage, vsum, vrecv, v_send, v_recv)
        sum_end(stage, v_copy, vsum, vrecv)

    def as_column(row):
        return jnp.sum(jnp.where(diagonal, row, 0.0), 1, keepdims=True)

    grad_r = w_r - as_column(vsum[steps, pl.ds(0, 1), pl.ds(0, modes)])
    grad_i = w_i - as_column(vsum[steps, pl.ds(8, 1), pl.ds(0, modes)])
    new_ref[pl.ds(0, 1), :] = exps_ref[pl.ds(0, 1), :] - jnp.sum(
        hinv_r * grad_r + hinv_i * grad_i, 0, keepdims=True
    )
    new_ref[pl.ds(1, 1), :] = exps_ref[pl.ds(1, 1), :] - jnp.sum(
        hinv_r * grad_i - hinv_i * grad_r, 0, keepdims=True
    )
    for out in outs:
        out.wait()
    for copy in sends:
        copy.wait_send()


def exchange(yz, gram, exponents, groups, spaces):
    modes = exponents.shape[1]
    double, columns = 2 * modes, yz.shape[1]
    tm_bits, sp_bits = groups.bit_length() - 1, spaces.bit_length() - 1
    assert groups == 2**tm_bits and spaces == 2**sp_bits
    parts = min(len(ORDERS), columns // (groups * LANES))
    steps = tm_bits + sp_bits
    width = columns // parts

    def buffer(*shape):
        return pltpu.VMEM(shape, jnp.float32)

    def dma(*shape):
        return pltpu.SemaphoreType.DMA(shape)

    vmem = pl.BlockSpec(memory_space=pltpu.VMEM)
    return pl.pallas_call(
        functools.partial(exchange_kernel, modes, tm_bits, sp_bits, parts),
        out_shape=(
            jax.ShapeDtypeStruct((double, columns), jnp.float32),
            jax.ShapeDtypeStruct(exponents.shape, jnp.float32),
        ),
        in_specs=[vmem] * 3,
        out_specs=(pl.BlockSpec(memory_space=pl.ANY), vmem),
        scratch_shapes=[
            buffer(double, columns),
            [buffer(parts, double, width >> (s + 1)) for s in range(tm_bits)],
            buffer(tm_bits + 1, double, LANES),
            buffer(tm_bits, double, LANES),
            buffer(steps + 1, double, LANES),
            buffer(steps, double, LANES),
            buffer(steps + 1, 16, LANES),
            buffer(steps, 16, LANES),
            dma(parts, tm_bits), dma(parts, tm_bits),
            dma(parts, tm_bits), dma(parts, tm_bits),
            dma(tm_bits), dma(tm_bits),
            dma(steps), dma(steps),
            dma(steps), dma(steps),
            dma(parts),
        ],
        compiler_params=pltpu.CompilerParams(
            collective_id=0, has_side_effects=True, vmem_limit_bytes=32 * 2**20
        ),
    )(yz, gram, exponents)


def shards(snapshots, exponents):
    local_rows, columns = snapshots.shape
    modes = exponents.shape[1]
    groups, spaces = lax.axis_size("tm"), lax.axis_size("space")
    rows = lax.axis_index("tm") * local_rows + jnp.arange(local_rows, dtype=jnp.int32)
    time = (rows.astype(jnp.float32) / (local_rows * groups))[:, None]
    magnitude = jnp.exp(time * exponents[0][None, :])
    phase_angle = time * exponents[1][None, :]
    real, imag = magnitude * jnp.cos(phase_angle), magnitude * jnp.sin(phase_angle)
    plain = jnp.concatenate([real, -imag], 1)
    basis_b = jnp.concatenate([plain, time * plain], 1).astype(jnp.bfloat16)
    yz = lax.dot_general(
        basis_b, snapshots, (((0,), (0,)), ((), ())), preferred_element_type=jnp.float32
    )
    both = jnp.concatenate([plain, jnp.concatenate([imag, real], 1)], 0)
    twice = jnp.concatenate([time, time], 0)
    first = both[:, :modes]
    gram_gc = exact_dot(both, jnp.concatenate([first, twice * first], 1), ((0,), (0,)))
    gram_e = exact_dot(twice * both, twice * first, ((0,), (0,)))
    gram = jnp.concatenate(
        [gram_gc, gram_e, jnp.zeros((2 * modes, LANES - 3 * modes), jnp.float32)], 1
    )
    amp_rows, new_exponents = exchange(yz, gram, exponents, groups, spaces)
    fitted = jnp.dot(
        basis_b[:, : 2 * modes],
        amp_rows.astype(jnp.bfloat16),
        preferred_element_type=jnp.float32,
    )
    residual = (snapshots.astype(jnp.float32) - fitted).astype(jnp.bfloat16)
    return (new_exponents, amp_rows.reshape(2, modes, columns), residual)


def solution(mesh):
    return jax.shard_map(
        shards,
        mesh=mesh,
        in_specs=(P("tm", "space"), P()),
        out_specs=(P(), P(None, None, "space"), P("tm", "space")),
        check_vma=False,
    )
```

```python
import functools

import jax
import jax.numpy as jnp
from jax import lax
from jax.experimental import pallas as pl
from jax.experimental.pallas import tpu as pltpu
from jax.sharding import PartitionSpec as P

damping = 0.01
MESH = pl.DeviceIdType.MESH
LANES = 128
WAVES = 2
TILE = 512
ORDERS = ((0, 1, 2), (1, 0, 2), (2, 0, 1), (1, 2, 0))


def phases_of(part, tm_bits):
    first = [b for b in ORDERS[part % len(ORDERS)] if b < tm_bits]
    order = first + [b for b in range(tm_bits) if b not in first]
    tail = order[2:]
    return [[b] for b in order[:2]] + [tail[i : i + 2] for i in range(0, len(tail), 2)]


def exact_dot(left, right, dims=((1,), (0,))):
    return lax.dot_general(
        left,
        right,
        (dims, ((), ())),
        precision=lax.Precision.HIGHEST,
        preferred_element_type=jnp.float32,
    )


def complex_inverse(real, imag):
    modes = real.shape[0]
    rows = lax.broadcasted_iota(jnp.int32, real.shape, 0)
    cols = lax.broadcasted_iota(jnp.int32, real.shape, 1)
    for k in range(modes):
        on_row, on_col = rows == k, cols == k
        scale = 1.0 / real[k : k + 1, k : k + 1]
        row_r = jnp.where(on_col[:1], 1.0, real[k : k + 1, :]) * scale
        row_i = jnp.where(on_col[:1], 0.0, imag[k : k + 1, :]) * scale
        col_r, col_i = real[:, k : k + 1], imag[:, k : k + 1]
        real = jnp.where(
            on_row, row_r, jnp.where(on_col, 0.0, real) - (col_r * row_r - col_i * row_i)
        )
        imag = jnp.where(
            on_row, row_i, jnp.where(on_col, 0.0, imag) - (col_r * row_i + col_i * row_r)
        )
    return real, imag


def complex_dot(ar, ai, br, bi):
    return exact_dot(ar, br) - exact_dot(ai, bi), exact_dot(ar, bi) + exact_dot(ai, br)


def exchange_kernel(
    modes, tm_bits, sp_bits, parts,
    x_ref, basis_ref, gram_ref, exps_ref,
    amp_ref, new_ref,
    xbuf, yz_ref, full, halves, gsum, grecv, ssum, srecv, vsum, vnear, vfar,
    rs_send, rs_recv, ag_send, ag_recv,
    g_send, g_recv, s_send, s_recv, n_send, n_recv, f_send, f_recv, x_sem, out_sem,
):
    double = 2 * modes
    columns = full.shape[1]
    width = columns // parts
    band = double // WAVES
    me, sp = lax.axis_index("tm"), lax.axis_index("space")
    swap = sp % 2

    def stride_of(bit):
        if tm_bits >= 2 and bit == 0:
            return 1 + swap
        if tm_bits >= 2 and bit == 1:
            return 2 - swap
        return 2**bit

    def flip(index, stride):
        side = (index // stride) % 2
        return side, index + (1 - 2 * side) * stride

    friends = [(flip(me, 2**b)[1], sp) for b in range(tm_bits)]
    friends += [(me, flip(sp, 2**b)[1]) for b in range(sp_bits)]

    spaces, low = 2**sp_bits, 2 ** (tm_bits // 2)
    n_near, n_far = low * spaces, 2**tm_bits // low
    near_slot, far_slot = (me % low) * spaces + sp, me // low
    near, far = [], []
    for d in range(1, n_near):
        other = (near_slot + d) % n_near
        near.append((far_slot * low + other // spaces, other % spaces))
    for d in range(1, n_far):
        far.append(((far_slot + d) % n_far * low + me % low, sp))

    def lanes(start, size):
        return pl.ds(pl.multiple_of(start, LANES), size)

    plan, mixed = [], set()
    for p in range(parts):
        plan.append([])
        for bits in phases_of(p, tm_bits):
            sides = [flip(me, stride_of(b))[0] for b in bits]
            mine = sum(side * 2**j for j, side in enumerate(sides))
            partners = []
            for mask in range(1, 2 ** len(bits)):
                device, place, chosen = me, mine, []
                for j, b in enumerate(bits):
                    if mask >> j & 1:
                        device = device + (1 - 2 * sides[j]) * stride_of(b)
                        place = place + (1 - 2 * sides[j]) * 2**j
                        chosen.append(b)
                partners.append((device, place))
                mixed.add(tuple(sorted(chosen)))
                mixed.add(tuple(sorted({0: 1, 1: 0}.get(b, b) for b in chosen)))
            plan[p].append((len(bits), mine, partners))
    extra = []
    for chosen in sorted(mixed):
        if min(chosen) < tm_bits // 2 <= max(chosen):
            device = me
            for b in chosen:
                device = device + (1 - 2 * ((me // 2**b) % 2)) * 2**b
            extra.append((device, sp))
    n_phases = len(plan[0])
    sizes = [width]
    for count, _, _ in plan[0]:
        sizes.append(sizes[-1] >> count)

    half = width // 2

    def part_half(p, k):
        side = plan[p][0][1]
        return (1 - side) * half if k == 0 else side * half

    loads = {}
    for k in range(2):
        for p in range(parts):
            at = part_half(p, k)
            loads[p, k] = pltpu.make_async_copy(
                x_ref.at[:, lanes(p * width + at, half)],
                xbuf.at[p, :, lanes(at, half)],
                x_sem.at[p, k],
            )
            loads[p, k].start()

    barrier = pltpu.get_barrier_semaphore()
    for friend in near + far + extra:
        pl.semaphore_signal(barrier, inc=1, device_id=friend, device_id_type=MESH)
    pl.semaphore_wait(barrier, len(near + far + extra))

    def project(p, k):
        loads[p, k].wait()
        at = part_half(p, k)
        tile = min(TILE, half)

        def step(i, carry):
            start = at + i * tile
            yz_ref[:, lanes(p * width + start, tile)] = jnp.dot(
                basis_ref[...],
                xbuf[p, :, lanes(start, tile)],
                preferred_element_type=jnp.float32,
            )
            return carry

        lax.fori_loop(0, half // tile, step, 0)

    def remote(src, dst, send, recv, friend):
        copy = pltpu.make_async_remote_copy(
            src_ref=src, dst_ref=dst, send_sem=send, recv_sem=recv,
            device_id=friend, device_id_type=MESH,
        )
        copy.start()
        return copy

    sends = []

    def sum_start(stage, total, landed, send, recv):
        copy = remote(
            total.at[stage], landed.at[stage], send.at[stage], recv.at[stage], friends[stage]
        )
        sends.append(copy)
        return copy

    def sum_end(stage, copy, total, landed):
        copy.wait_recv()
        total[stage + 1] = total[stage] + landed[stage]

    def scatter_start(p, h, s):
        size = sizes[s + 1]
        rows = pl.ds(h * band, band)
        copies = []
        for m, (device, place) in enumerate(plan[p][s][2]):
            if s == 0:
                src = yz_ref.at[rows, lanes(p * width + place * size, size)]
            else:
                src = halves[s - 1].at[p, 0, rows, lanes(place * size, size)]
            copies.append(
                remote(
                    src, halves[s].at[p, m, rows, :],
                    rs_send.at[p, h, s, m], rs_recv.at[p, h, s, m], (device, sp),
                )
            )
        sends.extend(copies)
        return copies

    def landed(copies):
        for copy in copies:
            copy.wait_recv()

    def scatter_add(p, h, s):
        size = sizes[s + 1]
        _, mine, partners = plan[p][s]
        rows = pl.ds(h * band, band)
        if s == 0:
            total = yz_ref[rows, lanes(p * width + mine * size, size)]
        else:
            total = halves[s - 1][p, 0, rows, lanes(mine * size, size)]
        for m in range(len(partners)):
            total = total + halves[s][p, m, rows, :]
        halves[s][p, 0, rows, :] = total

    gsum[0] = gram_ref[...]
    g_copy = sum_start(0, gsum, grecv, g_send, g_recv)
    flying = {}
    for p in range(parts):
        project(p, 0)
        for h in range(WAVES):
            flying[p, h] = scatter_start(p, h, 0)
    for p in range(parts):
        project(p, 1)
    for s in range(tm_bits):
        sum_end(s, g_copy, gsum, grecv)
        if s + 1 < tm_bits:
            g_copy = sum_start(s + 1, gsum, grecv, g_send, g_recv)
        if s + 1 < n_phases:
            for h in range(WAVES):
                for p in range(parts):
                    landed(flying[p, h])
                    scatter_add(p, h, s)
                    flying[p, h] = scatter_start(p, h, s + 1)

    blocks = gsum[tm_bits]

    def block(index):
        moved = blocks if index == 0 else pltpu.roll(blocks, LANES - index * modes, 1)
        return moved[:modes, :modes], moved[modes:, :modes]

    g_r, g_i = block(0)
    c_r, c_i = block(1)
    e_r, e_i = block(2)
    inv_r, inv_i = complex_inverse(g_r, g_i)
    offsets = []
    last = n_phases - 1

    def gather_start(p, h, s):
        where = full.at[pl.ds(h * band, band), lanes(offsets[p], sizes[s + 1])]
        copies = [
            remote(
                where, where, ag_send.at[p, h, s, m], ag_recv.at[p, h, s, m], (device, sp)
            )
            for m, (device, _) in enumerate(plan[p][s][2])
        ]
        sends.extend(copies)
        return copies

    owned = []
    for p in range(parts):
        for h in range(WAVES):
            landed(flying[p, h])
            scatter_add(p, h, last)
        owned.append(halves[last][p, 0])
        offsets.append(p * width + sum(plan[p][s][1] * sizes[s + 1] for s in range(n_phases)))
    owned = jnp.concatenate(owned, 1)
    own_r, own_i = complex_dot(inv_r, inv_i, owned[:modes], owned[modes:])
    for p in range(parts):
        size = sizes[-1]
        full[pl.ds(0, modes), lanes(offsets[p], size)] = own_r[:, p * size : (p + 1) * size]
        full[pl.ds(modes, modes), lanes(offsets[p], size)] = own_i[:, p * size : (p + 1) * size]
        for h in range(WAVES):
            flying[p, h] = gather_start(p, h, last)
    over = ((1,), (1,))
    self_r = exact_dot(own_r, own_r, over) + exact_dot(own_i, own_i, over)
    self_i = exact_dot(own_r, own_i, over) - exact_dot(own_i, own_r, over)

    ssum[0] = jnp.zeros(ssum.shape[1:], jnp.float32)
    ssum[0, pl.ds(0, modes), pl.ds(0, modes)] = self_r
    ssum[0, pl.ds(modes, modes), pl.ds(0, modes)] = self_i
    s_copy = sum_start(0, ssum, srecv, s_send, s_recv)
    s_stage = 0
    steps = len(friends)
    t_r, t_i = complex_dot(inv_r, inv_i, c_r, c_i)
    u_r, u_i = complex_dot(c_r, c_i, t_r, t_i)
    m_r, m_i = e_r - u_r, e_i - u_i
    for s in range(last, 0, -1):
        for p in range(parts):
            offsets[p] = offsets[p] - plan[p][s][1] * sizes[s + 1]
        for h in range(WAVES):
            for p in range(parts):
                landed(flying[p, h])
                flying[p, h] = gather_start(p, h, s - 1)
        sum_end(s_stage, s_copy, ssum, srecv)
        s_stage += 1
        s_copy = sum_start(s_stage, ssum, srecv, s_send, s_recv)
    while s_stage < steps:
        sum_end(s_stage, s_copy, ssum, srecv)
        s_stage += 1
        if s_stage < steps:
            s_copy = sum_start(s_stage, ssum, srecv, s_send, s_recv)

    s_r = ssum[steps, pl.ds(0, modes), pl.ds(0, modes)]
    s_i = ssum[steps, pl.ds(modes, modes), pl.ds(0, modes)]
    square = (modes, modes)
    diagonal = lax.broadcasted_iota(jnp.int32, square, 0) == lax.broadcasted_iota(
        jnp.int32, square, 1
    )
    h_r = s_r * m_r - s_i * m_i + jnp.where(diagonal, damping, 0.0)
    h_i = s_r * m_i + s_i * m_r
    hinv_r, hinv_i = complex_inverse(h_r, h_i)
    w_r = jnp.sum(c_r * s_r - c_i * s_i, 1, keepdims=True)
    w_i = jnp.sum(c_r * s_i + c_i * s_r, 1, keepdims=True)

    v_r = jnp.zeros((modes, LANES), jnp.float32)
    v_i = jnp.zeros((modes, LANES), jnp.float32)
    outs = []
    for p in range(parts):
        for h in range(WAVES):
            landed(flying[p, h])
        part = pl.ds(p * width, width)
        out = pltpu.make_async_copy(full.at[:, part], amp_ref.at[:, part], out_sem.at[p])
        out.start()
        outs.append(out)
        run = 4

        def step(i, carry, p=p):
            v_r, v_i = carry
            for j in range(run):
                at = lanes(p * width + (i * run + j) * LANES, LANES)
                a_r, a_i = full[pl.ds(0, modes), at], full[pl.ds(modes, modes), at]
                z_r = yz_ref[pl.ds(double, modes), at]
                z_i = yz_ref[pl.ds(double + modes, modes), at]
                v_r = v_r + (a_r * z_r + a_i * z_i)
                v_i = v_i + (a_r * z_i - a_i * z_r)
            return v_r, v_i

        v_r, v_i = lax.fori_loop(0, width // (run * LANES), step, (v_r, v_i))

    ones = jnp.ones((8, LANES), jnp.float32)

    def gather_sum(stage, slots, slot, peers, send, recv):
        copies = []
        for d, peer in enumerate(peers):
            copy = remote(vsum.at[stage], slots.at[slot], send.at[d], recv.at[d], peer)
            copies.append(copy)
            sends.append(copy)
        slots[slot] = vsum[stage]
        for copy in copies:
            copy.wait_recv()
        total = slots[0]
        for k in range(1, len(peers) + 1):
            total = total + slots[k]
        return total

    vsum[0] = jnp.zeros(vsum.shape[1:], jnp.float32)
    vsum[0, :, pl.ds(0, double)] = exact_dot(
        ones, jnp.concatenate([v_r, v_i], 0), ((1,), (1,))
    )
    vsum[1] = gather_sum(0, vnear, near_slot, near, n_send, n_recv)
    v_all = gather_sum(1, vfar, far_slot, far, f_send, f_recv)[:1]

    wide = (modes, LANES)
    spread = lax.broadcasted_iota(jnp.int32, wide, 1) - lax.broadcasted_iota(jnp.int32, wide, 0)

    def as_column(shift):
        return jnp.sum(jnp.where(spread == shift, v_all, 0.0), 1, keepdims=True)

    grad_r = w_r - as_column(0)
    grad_i = w_i - as_column(modes)
    new_ref[pl.ds(0, 1), :] = exps_ref[pl.ds(0, 1), :] - jnp.sum(
        hinv_r * grad_r + hinv_i * grad_i, 0, keepdims=True
    )
    new_ref[pl.ds(1, 1), :] = exps_ref[pl.ds(1, 1), :] - jnp.sum(
        hinv_r * grad_i - hinv_i * grad_r, 0, keepdims=True
    )
    for out in outs:
        out.wait()
    for copy in sends:
        copy.wait_send()


def exchange(snapshots, basis_b, gram, exponents, groups, spaces):
    modes = exponents.shape[1]
    double = 2 * modes
    local_rows, columns = snapshots.shape
    tm_bits, sp_bits = groups.bit_length() - 1, spaces.bit_length() - 1
    assert groups == 2**tm_bits and spaces == 2**sp_bits
    parts = min(len(ORDERS), columns // (groups * LANES))
    steps = tm_bits + sp_bits
    width = columns // parts
    low = 2 ** (tm_bits // 2)
    counts = [len(bits) for bits in phases_of(0, tm_bits)]
    copies = (parts, WAVES, len(counts), 2 ** max(counts) - 1)
    near, far = low * spaces, groups // low

    def buffer(*shape):
        return pltpu.VMEM(shape, jnp.float32)

    def dma(*shape):
        return pltpu.SemaphoreType.DMA(shape)

    vmem = pl.BlockSpec(memory_space=pltpu.VMEM)
    return pl.pallas_call(
        functools.partial(exchange_kernel, modes, tm_bits, sp_bits, parts),
        out_shape=(
            jax.ShapeDtypeStruct((double, columns), jnp.float32),
            jax.ShapeDtypeStruct(exponents.shape, jnp.float32),
        ),
        in_specs=[pl.BlockSpec(memory_space=pl.ANY)] + [vmem] * 3,
        out_specs=(pl.BlockSpec(memory_space=pl.ANY), vmem),
        scratch_shapes=[
            pltpu.VMEM((parts, local_rows, width), snapshots.dtype),
            buffer(2 * double, columns),
            buffer(double, columns),
            [
                buffer(parts, 2**count - 1, double, width >> sum(counts[: s + 1]))
                for s, count in enumerate(counts)
            ],
            buffer(tm_bits + 1, double, LANES),
            buffer(tm_bits, double, LANES),
            buffer(steps + 1, double, LANES),
            buffer(steps, double, LANES),
            buffer(2, 8, LANES),
            buffer(near, 8, LANES),
            buffer(far, 8, LANES),
            dma(*copies), dma(*copies),
            dma(*copies), dma(*copies),
            dma(tm_bits), dma(tm_bits),
            dma(steps), dma(steps),
            dma(near - 1), dma(near - 1),
            dma(far - 1), dma(far - 1),
            dma(parts, 2),
            dma(parts),
        ],
        compiler_params=pltpu.CompilerParams(
            collective_id=0, has_side_effects=True, vmem_limit_bytes=40 * 2**20
        ),
    )(snapshots, basis_b, gram, exponents)


def shards(snapshots, exponents):
    local_rows, columns = snapshots.shape
    modes = exponents.shape[1]
    groups, spaces = lax.axis_size("tm"), lax.axis_size("space")
    rows = lax.axis_index("tm") * local_rows + jnp.arange(local_rows, dtype=jnp.int32)
    time = (rows.astype(jnp.float32) / (local_rows * groups))[None, :]
    magnitude = jnp.exp(time * exponents[0][:, None])
    phase_angle = time * exponents[1][:, None]
    real, imag = magnitude * jnp.cos(phase_angle), magnitude * jnp.sin(phase_angle)
    plain = jnp.concatenate([real, -imag], 0)
    basis_b = jnp.concatenate([plain, time * plain], 0).astype(jnp.bfloat16)
    both = jnp.concatenate([plain, jnp.concatenate([imag, real], 0)], 1)
    twice = jnp.concatenate([time, time], 1)
    first = both[:modes]
    over = ((1,), (1,))
    gram_gc = exact_dot(both, jnp.concatenate([first, twice * first], 0), over)
    gram_e = exact_dot(twice * both, twice * first, over)
    gram = jnp.concatenate(
        [gram_gc, gram_e, jnp.zeros((2 * modes, LANES - 3 * modes), jnp.float32)], 1
    )
    amp_rows, new_exponents = exchange(snapshots, basis_b, gram, exponents, groups, spaces)
    fitted = lax.dot_general(
        basis_b[: 2 * modes],
        amp_rows.astype(jnp.bfloat16),
        (((0,), (0,)), ((), ())),
        preferred_element_type=jnp.float32,
    )
    residual = (snapshots.astype(jnp.float32) - fitted).astype(jnp.bfloat16)
    return (new_exponents, amp_rows.reshape(2, modes, columns), residual)


def solution(mesh):
    return jax.shard_map(
        shards,
        mesh=mesh,
        in_specs=(P("tm", "space"), P()),
        out_specs=(P(), P(None, None, "space"), P("tm", "space")),
        check_vma=False,
    )
```
